32 devices in a mesh: wa: 4 (over y, core), row: 8 (over z, x).
Axes of the slice: x: 2, y: 2, z: 4, core: 2. Of those that a mesh axis runs over, the one named last changes fastest.
Arguments:
- activations: bfloat16 [24, 1280, 512], P('row', 'wa'), may hold values from -1300 to 1300, as said below
- gain_one: float32 [1280], P('wa'), may hold values from 0.1 to 1.9
- shift_one: float32 [1280], P('wa'), may hold values from -3 to 3
- kernel_one: bfloat16 [3, 3, 8, 4, 51200], P(None, None, 'row', 'wa'), may hold values from -0.0546875 to 0.0546875
- bias_one: float32 [1280], P('wa'), may hold values from -3 to 3
- gain_two: float32 [1280], P('wa'), may hold values from 0.1 to 1.9
- shift_two: float32 [1280], P('wa'), may hold values from -3 to 3
- kernel_two: bfloat16 [3, 3, 8, 4, 51200], P(None, None, 'row', 'wa'), may hold values from -0.0546875 to 0.0546875
- bias_two: float32 [1280], P('wa'), may hold values from -3 to 3
Outputs:
- result: bfloat16 [24, 1280, 512], P('row', 'wa')
The draws below stay inside these ranges and needn't reach their ends.
Inputs may be any that keep to these rules, and one draw needn't show every extreme that they name: `activations`: real-valued feature maps whose magnitude differs from pixel row to pixel row, from pixel to pixel and from channel to channel.
All inputs are finite; a program needn't handle non-finite values.
Results may differ from the reference program's by a relative error of at most 0.0056.
Values may be sent and summed in bfloat16 or wider, within the bound.
No kernel may reach another device: no remote copies, remote signals or barrier semaphores. Data moves between devices by JAX's collectives and lax.ppermute only.
A program may use at most 128 MiB of HBM per device.

```python
import math
import jax
import jax.numpy as jnp
from jax import lax

C = 1280
GROUPS = 32
WIDTH = 32
IMAGES = 16
HEIGHT = 24
CI_DEV = 160
CO_DEV = 320
N_WA = 4
N_ROW = 8


def draw_activations(key, part):
    key_base, key_rows, key_chan, key_pixel = jax.random.split(key, 4)
    shape_full = (HEIGHT, C, IMAGES * WIDTH)
    position = jnp.arange(HEIGHT, dtype=jnp.float32) / max(HEIGHT - 1, 1)
    base = jnp.clip(jax.random.normal(key_base, shape_full, jnp.float32), -6.0, 6.0)
    ramp = jnp.exp(position * math.log(3.0))
    row_factor = jnp.exp(jax.random.uniform(key_rows, (HEIGHT,), jnp.float32, 0.0, math.log(3.5)))
    chan_factor = jnp.exp(jax.random.uniform(key_chan, (C,), jnp.float32, 0.0, math.log(10.0)))
    pixel_factor = jnp.exp(jax.random.uniform(key_pixel, (HEIGHT, IMAGES * WIDTH), jnp.float32, 0.0, math.log(2.0)))
    scaled = base * (ramp * row_factor)[:, None, None] * pixel_factor[:, None, :] * chan_factor[None, :, None]
    return scaled.astype(jnp.bfloat16)


def level_of(own_key, shape, cuts, least, high):
    level = 1.0
    for dim, blocks in cuts:
        heights = jax.random.uniform(jax.random.fold_in(jax.random.fold_in(own_key, 6), dim), (blocks,), jnp.float32, least / len(cuts), high / len(cuts))
        level = level * jnp.repeat(jnp.exp(heights), shape[dim] // blocks).reshape((-1,) + (1,) * (len(shape) - 1 - dim))
    return level


def scatter_about(own_key, shape, width, reach, shards=(), kind=jnp.bfloat16):
    entries = width * jax.random.normal(own_key, shape, jnp.float32)
    if shards:
        entries = entries * level_of(own_key, shape, shards, -0.22, 0.18)
    return jnp.clip(entries, -reach, reach).astype(kind)


def setup_inputs(seed: int = 0) -> dict:
    seeds = jax.random.split(jax.random.key(seed), 10)
    return {
        "activations": draw_activations(jax.random.fold_in(seeds[9], 71), 0),
        "gain_one": jnp.clip(1.0 + 0.18 * jax.random.normal(seeds[1], (C,), jnp.float32), 0.1, 1.9),
        "shift_one": scatter_about(seeds[2], (C,), 0.5, 3.0, ((0, 4),), jnp.float32),
        "kernel_one": scatter_about(seeds[3], (3, 3, N_ROW, N_WA, CI_DEV * CO_DEV), (9 * C) ** -0.5, 0.0546875, ((2, 8), (3, 4))),
        "bias_one": scatter_about(seeds[4], (C,), 0.5, 3.0, ((0, 4),), jnp.float32),
        "gain_two": jnp.clip(1.0 + 0.18 * jax.random.normal(seeds[5], (C,), jnp.float32), 0.1, 1.9),
        "shift_two": scatter_about(seeds[6], (C,), 0.5, 3.0, ((0, 4),), jnp.float32),
        "kernel_two": scatter_about(seeds[7], (3, 3, N_ROW, N_WA, CI_DEV * CO_DEV), (9 * C) ** -0.5, 0.0546875, ((2, 8), (3, 4))),
        "bias_two": scatter_about(seeds[8], (C,), 0.5, 3.0, ((0, 4),), jnp.float32),
    }


def unblock(kernel):
    shaped = kernel.reshape(3, 3, N_ROW, N_WA, C // N_ROW, C // N_WA)
    return jnp.transpose(shaped, (0, 1, 2, 4, 3, 5)).reshape(3, 3, C, C)

def normalize(field, gain, shift):
    height, channels, columns = field.shape
    grouped = field.reshape(height, GROUPS, channels // GROUPS, IMAGES, WIDTH)
    center = lax.optimization_barrier(jnp.mean(grouped, axis=(0, 2, 4), keepdims=True))
    spread = lax.optimization_barrier(jnp.mean(jnp.square(grouped - center), axis=(0, 2, 4), keepdims=True))
    normed = ((grouped - center) * lax.rsqrt(spread + 1e-05)).reshape(height, channels, columns)
    return jax.nn.silu(normed * gain[:, None] + shift[:, None]).astype(jnp.bfloat16)

def convolve(panel, kernel, bias):
    height, channels, columns = panel.shape
    split = panel.reshape(height, channels, IMAGES, WIDTH)
    padded = jnp.pad(split, ((1, 1), (0, 0), (0, 0), (1, 1)))
    full = unblock(kernel)
    total = jnp.zeros((height, full.shape[3], IMAGES, WIDTH), jnp.float32)
    for row_tap in range(3):
        for col_tap in range(3):
            window = padded[row_tap:row_tap + height, :, :, col_tap:col_tap + WIDTH].astype(jnp.float32)
            total = total + jnp.einsum('hciw,co->hoiw', window, full[row_tap, col_tap].astype(jnp.float32))
    return total.reshape(height, full.shape[3], columns) + bias[None, :, None]

def reference(activations, gain_one, shift_one, kernel_one, bias_one, gain_two, shift_two, kernel_two, bias_two):
    first = normalize(activations.astype(jnp.float32), gain_one, shift_one)
    hidden = convolve(first, kernel_one, bias_one).astype(jnp.bfloat16)
    second = normalize(hidden.astype(jnp.float32), gain_two, shift_two)
    return convolve(second, kernel_two, bias_two).astype(jnp.bfloat16)
```

```python
import jax
import jax.numpy as jnp
from jax import lax
from jax.experimental import pallas as pl
from jax.experimental.pallas import tpu as pltpu
from jax.sharding import PartitionSpec as P

C = 1280
GROUPS = 32
WIDTH = 32
GROUP_SIZE = C // GROUPS
TAPS = 3
EPS = 1e-05
VMEM_LIMIT = 60 * 1024 * 1024


def params(**extra):
    return pltpu.CompilerParams(vmem_limit_bytes=VMEM_LIMIT, **extra)


def xor_pairs(count, bit):
    return [(i, i ^ bit) for i in range(count)]


def spread_in_image(value):
    lane = lax.broadcasted_iota(jnp.int32, value.shape, 1)
    lanes = value.shape[1]
    step = 1
    while step < WIDTH:
        above = pltpu.roll(value, lanes - step, 1)
        below = pltpu.roll(value, step, 1)
        value = value + jnp.where((lane & step) == 0, above, below)
        step *= 2
    return value


def stats_body(x_ref, out_ref):
    rows, chans, lanes = x_ref.shape
    groups = chans // GROUP_SIZE
    count = rows * GROUP_SIZE * WIDTH
    for g in range(groups):
        part = x_ref[:, g * GROUP_SIZE : (g + 1) * GROUP_SIZE, :].astype(jnp.float32)
        total = jnp.sum(jnp.sum(part, axis=0), axis=0, keepdims=True)
        mean = spread_in_image(total) / count
        off = part - mean[None]
        square = jnp.sum(jnp.sum(off * off, axis=0), axis=0, keepdims=True)
        out_ref[0, g : g + 1, :] = mean
        out_ref[1, g : g + 1, :] = spread_in_image(square)


def local_stats(x):
    groups = x.shape[1] // GROUP_SIZE
    return pl.pallas_call(
        stats_body,
        out_shape=jax.ShapeDtypeStruct((2, groups, x.shape[2]), jnp.float32),
        compiler_params=params(),
        name="stats",
    )(x)


def combined_stats(stats, count):
    n_row = lax.axis_size("row")
    bit = 1
    while bit < n_row:
        other = lax.ppermute(stats, "row", xor_pairs(n_row, bit))
        delta = other[0] - stats[0]
        mean = 0.5 * (stats[0] + other[0])
        square = stats[1] + other[1] + delta * delta * (0.5 * count)
        stats = jnp.stack([mean, square])
        count *= 2
        bit *= 2
    return stats, count


def norm_body(count, x_ref, stats_ref, gain_ref, shift_ref, out_ref):
    rows, chans, lanes = x_ref.shape
    groups = chans // GROUP_SIZE
    for g in range(groups):
        span = slice(g * GROUP_SIZE, (g + 1) * GROUP_SIZE)
        mean = stats_ref[0, g : g + 1, :]
        scale = lax.rsqrt(stats_ref[1, g : g + 1, :] / count + EPS)
        gain = gain_ref[span, :]
        shift = shift_ref[span, :]
        for r in range(rows):
            v = (x_ref[r, span, :].astype(jnp.float32) - mean) * scale * gain + shift
            out_ref[r, span, :] = (v / (1.0 + jnp.exp(-v))).astype(jnp.bfloat16)


def activate(x, gain, shift):
    count = x.shape[0] * GROUP_SIZE * WIDTH
    stats, count = combined_stats(local_stats(x), count)
    return pl.pallas_call(
        lambda *refs: norm_body(count, *refs),
        out_shape=jax.ShapeDtypeStruct(x.shape, jnp.bfloat16),
        compiler_params=params(),
        name="norm",
    )(x, stats, gain[:, None], shift[:, None])


def gather_wa(x):
    n_wa = lax.axis_size("wa")
    pieces = {0: x}
    bit = n_wa // 2
    while bit:
        for k in sorted(pieces):
            pieces[k | bit] = lax.ppermute(pieces[k], "wa", xor_pairs(n_wa, bit))
        bit //= 2
    return [pieces[k] for k in range(n_wa)]


def edges_of(x):
    n_row = lax.axis_size("row")
    above = lax.ppermute(x[-1:], "row", [(i, i + 1) for i in range(n_row - 1)])
    below = lax.ppermute(x[:1], "row", [(i + 1, i) for i in range(n_row - 1)])
    return jnp.concatenate([above, below], axis=0)


def prepared(kernel, ci, co):
    flat = kernel.reshape(TAPS, TAPS * ci, co)
    turned = jnp.transpose(flat, (2, 0, 1))
    depth = -(-TAPS * ci // 128) * 128
    turned = jnp.pad(turned, ((0, 0), (0, 0), (0, depth - TAPS * ci)))
    return turned.reshape(co, TAPS * depth)


def ring_order(n):
    return list(range(0, n, 2)) + list(range(n - 1, 0, -2))


def block_at(place, n):
    place = place % n
    return jnp.where(2 * place < n, 2 * place, 2 * (n - place) - 1)


def ring(own):
    n = lax.axis_size("row")
    r = lax.axis_index("row")
    place = jnp.where(r % 2 == 0, r // 2, n - 1 - r // 2)
    order = ring_order(n)
    up = [(order[i], order[(i + 1) % n]) for i in range(n)]
    down = [(d, s) for s, d in up]
    rounds = [([own], [block_at(place, n)])]
    a = b = own
    for s in range(1, n // 2):
        a = lax.ppermute(a, "row", up)
        b = lax.ppermute(b, "row", down)
        rounds.append(([a, b], [block_at(place - s, n), block_at(place + s, n)]))
    half = own.shape[0] // 2
    a = lax.ppermute(a[:half], "row", up)
    b = lax.ppermute(b[half:], "row", down)
    rounds.append(([a, b], [block_at(place + n // 2, n)]))
    return rounds


def conv_body(n_chunks, n_wa, split, final, idx_ref, *refs):
    refs = list(refs)
    n_arrays = 2 if split else n_chunks
    chunk_refs = [refs.pop(0) for _ in range(n_arrays)]
    body_refs = [refs.pop(0) for _ in range(n_wa)]
    edge_refs = [refs.pop(0) for _ in range(n_wa)]
    acc_ref = refs.pop(0)
    bias_ref = refs.pop(0) if final else None
    out_ref, wbuf, abuf, xbuf, wsem, asem = refs
    rows, co, lanes = out_ref.shape
    ci = abuf.shape[2]
    depth = xbuf.shape[1]
    per_shard = body_refs[0].shape[1] // ci
    me = idx_ref[n_chunks]

    def weight_copies(c):
        if split:
            half = co // 2
            return [
                pltpu.make_async_copy(ref, wbuf.at[c, pl.ds(i * half, half), :], wsem.at[i])
                for i, ref in enumerate(chunk_refs)
            ]
        return [pltpu.make_async_copy(chunk_refs[c], wbuf.at[c], wsem.at[c])]

    for c in range(n_chunks):
        for copy in weight_copies(c):
            copy.start()
        block = idx_ref[c]
        piece = (block // per_shard) ^ me
        offset = pl.multiple_of((block % per_shard) * ci, 16)
        for k in range(n_wa):

            @pl.when(piece == k)
            def _():
                pltpu.make_async_copy(
                    body_refs[k].at[:, pl.ds(offset, ci), :], abuf.at[c, pl.ds(1, rows)], asem.at[c, 0]
                ).start()
                pltpu.make_async_copy(
                    edge_refs[k].at[pl.ds(0, 1), pl.ds(offset, ci), :], abuf.at[c, pl.ds(0, 1)], asem.at[c, 1]
                ).start()
                pltpu.make_async_copy(
                    edge_refs[k].at[pl.ds(1, 1), pl.ds(offset, ci), :], abuf.at[c, pl.ds(rows + 1, 1)], asem.at[c, 2]
                ).start()

    if depth > TAPS * ci:
        xbuf[:, TAPS * ci :, :] = jnp.zeros((rows + 2, depth - TAPS * ci, lanes), jnp.bfloat16)
    column = lax.broadcasted_iota(jnp.int32, (ci, lanes), 1) % WIDTH

    def step(c, carry):
        pltpu.make_async_copy(
            body_refs[0].at[:, pl.ds(0, ci), :], abuf.at[c, pl.ds(1, rows)], asem.at[c, 0]
        ).wait()
        pltpu.make_async_copy(
            edge_refs[0].at[pl.ds(0, 1), pl.ds(0, ci), :], abuf.at[c, pl.ds(0, 1)], asem.at[c, 1]
        ).wait()
        pltpu.make_async_copy(
            edge_refs[0].at[pl.ds(1, 1), pl.ds(0, ci), :], abuf.at[c, pl.ds(rows + 1, 1)], asem.at[c, 2]
        ).wait()
        for r in range(rows + 2):
            v = abuf[c, r]
            zero = jnp.zeros_like(v)
            xbuf[r, 0:ci, :] = jnp.where(column == 0, zero, pltpu.roll(v, 1, 1))
            xbuf[r, ci : 2 * ci, :] = v
            xbuf[r, 2 * ci : 3 * ci, :] = jnp.where(column == WIDTH - 1, zero, pltpu.roll(v, lanes - 1, 1))
        if split:
            for copy in weight_copies(0):
                copy.wait()
        else:
            pltpu.make_async_copy(chunk_refs[0], wbuf.at[c], wsem.at[c]).wait()
        for r in range(rows):
            panel = xbuf[r : r + TAPS].reshape(TAPS * depth, lanes)
            acc_ref[r] += jnp.dot(wbuf[c], panel, preferred_element_type=jnp.float32)
        return carry

    for_all = step
    lax.fori_loop(0, n_chunks, for_all, 0)


def conv_part(rounds, pieces, edges, acc, bias, final):
    n_wa = lax.axis_size("wa")
    split = len(rounds) == 1 and len(rounds[0][0]) == 2 and len(rounds[0][1]) == 1
    chunks = [c for chunk_list, _ in rounds for c in chunk_list]
    blocks = [b for _, block_list in rounds for b in block_list]
    n_chunks = len(blocks)
    idx = jnp.stack([jnp.asarray(b, jnp.int32) for b in blocks] + [lax.axis_index("wa").astype(jnp.int32)])
    rows, chans, lanes = pieces[0].shape
    co = chunks[0].shape[0] * (2 if split else 1)
    kdim = chunks[0].shape[1]
    depth = kdim // TAPS
    ci = C // lax.axis_size("row")

    def body(idx_ref, *refs):
        refs = list(refs)
        n_in = len(chunks) + 2 * n_wa
        given = refs[:n_in]
        rest = refs[n_in:]
        acc_in = rest.pop(0) if acc is not None else None
        bias_ref = rest.pop(0) if final else None
        out_ref = rest.pop(0)
        if final:
            acc_ref = rest.pop(0)
        else:
            acc_ref = out_ref
        if acc_in is None:
            acc_ref[...] = jnp.zeros(acc_ref.shape, jnp.float32)
        else:
            acc_ref[...] = acc_in[...]
        conv_body(n_chunks, n_wa, split, False, idx_ref, *given, acc_ref, out_ref, *rest)
        if final:
            out_ref[...] = (acc_ref[...] + bias_ref[...][None]).astype(jnp.bfloat16)

    any_spec = pl.BlockSpec(memory_space=pl.ANY)
    full = pl.BlockSpec(memory_space=pltpu.VMEM)
    in_specs = [pl.BlockSpec(memory_space=pltpu.SMEM)] + [any_spec] * (len(chunks) + 2 * n_wa)
    args = [idx] + chunks + list(pieces) + list(edges)
    if acc is not None:
        in_specs.append(full)
        args.append(acc)
    if final:
        in_specs.append(full)
        args.append(bias[:, None])
    scratch = [pltpu.VMEM((rows, co, lanes), jnp.float32)] if final else []
    scratch += [
        pltpu.VMEM((n_chunks, co, kdim), jnp.bfloat16),
        pltpu.VMEM((n_chunks, rows + 2, ci, lanes), jnp.bfloat16),
        pltpu.VMEM((rows + 2, depth, lanes), jnp.bfloat16),
        pltpu.SemaphoreType.DMA((max(n_chunks, 2),)),
        pltpu.SemaphoreType.DMA((n_chunks, 3)),
    ]
    out_type = jnp.bfloat16 if final else jnp.float32
    return pl.pallas_call(
        body,
        in_specs=in_specs,
        out_specs=full,
        out_shape=jax.ShapeDtypeStruct((rows, co, lanes), out_type),
        scratch_shapes=scratch,
        compiler_params=params(),
        name="conv",
    )(*args)


def convolve(x, rounds, bias):
    pieces = gather_wa(x)
    edges = gather_wa(edges_of(x))
    n = len(rounds)
    cuts = [(0, n - 2), (n - 2, n - 1), (n - 1, n)]
    acc = None
    for first, last in cuts:
        acc = conv_part(rounds[first:last], pieces, edges, acc, bias, last == n)
    return acc


def per_device(
    activations,
    gain_one,
    shift_one,
    kernel_one,
    bias_one,
    gain_two,
    shift_two,
    kernel_two,
    bias_two,
):
    co = activations.shape[1]
    ci = kernel_one.shape[4] // co
    own_one = prepared(kernel_one, ci, co)
    own_two = prepared(kernel_two, ci, co)
    rounds_one = ring(own_one)
    own_two, _ = lax.optimization_barrier((own_two, rounds_one[-1][0]))
    rounds_two = ring(own_two)
    first = activate(activations, gain_one, shift_one)
    hidden = convolve(first, rounds_one, bias_one)
    second = activate(hidden, gain_two, shift_two)
    return convolve(second, rounds_two, bias_two)


def solution(mesh):
    placed = (
        P("row", "wa", None),
        P("wa"),
        P("wa"),
        P(None, None, "row", "wa", None),
        P("wa"),
        P("wa"),
        P("wa"),
        P(None, None, "row", "wa", None),
        P("wa"),
    )
    return jax.shard_map(
        per_device, mesh=mesh, in_specs=placed, out_specs=P("row", "wa", None), check_vma=False
    )
```

```python
import jax
import jax.numpy as jnp
from jax import lax
from jax.experimental import pallas as pl
from jax.experimental.pallas import tpu as pltpu
from jax.sharding import PartitionSpec as P


C = 1280
GROUPS = 32
WIDTH = 32
GROUP_SIZE = C // GROUPS
TAPS = 3
EPS = 1e-05
VMEM_LIMIT = 60 * 1024 * 1024


def params(**extra):
    return pltpu.CompilerParams(vmem_limit_bytes=VMEM_LIMIT, **extra)


def xor_pairs(count, bit):
    return [(i, i ^ bit) for i in range(count)]


def image_select(lanes, images=128):
    lane = lax.broadcasted_iota(jnp.int32, (lanes, images), 0) // WIDTH
    return (lane == lax.broadcasted_iota(jnp.int32, (lanes, images), 1)).astype(jnp.float32)


def image_sum(value, select):
    return jnp.dot(value, select, precision=lax.Precision.HIGHEST, preferred_element_type=jnp.float32)


def image_spread(value, select):
    return lax.dot_general(
        value, select, (((1,), (1,)), ((), ())), precision=lax.Precision.HIGHEST, preferred_element_type=jnp.float32
    )


def stats_body(x_ref, out_ref, total_ref):
    rows, chans, lanes = x_ref.shape
    groups = chans // GROUP_SIZE
    count = rows * GROUP_SIZE * WIDTH
    select = image_select(lanes)
    spans = [slice(g * GROUP_SIZE, (g + 1) * GROUP_SIZE) for g in range(groups)]
    for g in range(groups):
        part = x_ref[:, spans[g], :].astype(jnp.float32)
        total_ref[g : g + 1, :] = jnp.sum(jnp.sum(part, axis=0), axis=0, keepdims=True)
    mean = image_sum(total_ref[...], select) / count
    out_ref[0] = mean
    wide = image_spread(mean, select)
    for g in range(groups):
        off = x_ref[:, spans[g], :].astype(jnp.float32) - wide[None, g : g + 1, :]
        total_ref[g : g + 1, :] = jnp.sum(jnp.sum(off * off, axis=0), axis=0, keepdims=True)
    out_ref[1] = image_sum(total_ref[...], select)


def local_stats(x):
    groups = x.shape[1] // GROUP_SIZE
    return pl.pallas_call(
        stats_body,
        out_shape=jax.ShapeDtypeStruct((2, groups, 128), jnp.float32),
        scratch_shapes=[pltpu.VMEM((groups, x.shape[2]), jnp.float32)],
        compiler_params=params(),
        name="stats",
    )(x)


def exchanged(stats):
    n_row = lax.axis_size("row")
    return [stats] + [lax.ppermute(stats, "row", xor_pairs(n_row, k)) for k in range(1, n_row)]


def norm_body(count, n_row, flag_ref, x_ref, above_ref, below_ref, gain_ref, shift_ref, *refs):
    stats_refs = refs[:n_row]
    out_refs = refs[n_row:]
    rows, chans, lanes = x_ref.shape
    groups = chans // GROUP_SIZE
    width = out_refs[0].shape[1]
    select = image_select(lanes)
    center = sum(ref[0] for ref in stats_refs) / n_row
    square = sum(ref[1] for ref in stats_refs) + count * sum(jnp.square(ref[0] - center) for ref in stats_refs)
    scale = lax.rsqrt(square / (count * n_row) + EPS)
    wide_center = image_spread(center, select)
    wide_scale = image_spread(scale, select)
    for g in range(groups):
        span = slice(g * GROUP_SIZE, (g + 1) * GROUP_SIZE)
        out_ref = out_refs[g * GROUP_SIZE // width]
        start = g * GROUP_SIZE % width
        mean = wide_center[g : g + 1, :]
        inv = wide_scale[g : g + 1, :]
        gain = gain_ref[span, :]
        shift = shift_ref[span, :]

        def act(value):
            v = (value.astype(jnp.float32) - mean) * inv * gain + shift
            return v / (1.0 + jnp.exp(-v))

        here = slice(start, start + GROUP_SIZE)
        out_ref[0, here, :] = (act(above_ref[0, span, :]) * flag_ref[0]).astype(jnp.bfloat16)
        for r in range(rows):
            out_ref[r + 1, here, :] = act(x_ref[r, span, :]).astype(jnp.bfloat16)
        out_ref[rows + 1, here, :] = (act(below_ref[0, span, :]) * flag_ref[1]).astype(jnp.bfloat16)


def edges_of(x):
    n_row = lax.axis_size("row")
    above = lax.ppermute(x[-1:], "row", [(i, i + 1) for i in range(n_row - 1)])
    below = lax.ppermute(x[:1], "row", [(i + 1, i) for i in range(n_row - 1)])
    return above, below


def surroundings(x):
    return edges_of(x), exchanged(local_stats(x))


def activate(x, around, gain, shift):
    n_row = lax.axis_size("row")
    rows, chans, lanes = x.shape
    ci = C // n_row
    count = rows * GROUP_SIZE * WIDTH
    (above, below), stats = around
    r = lax.axis_index("row")
    flags = jnp.stack([r > 0, r < n_row - 1]).astype(jnp.float32)
    vmem = pl.BlockSpec(memory_space=pltpu.VMEM)
    return pl.pallas_call(
        lambda *refs: norm_body(count, n_row, *refs),
        in_specs=[pl.BlockSpec(memory_space=pltpu.SMEM)] + [vmem] * (5 + n_row),
        out_shape=[jax.ShapeDtypeStruct((rows + 2, ci, lanes), jnp.bfloat16)] * (chans // ci),
        compiler_params=params(),
        name="norm",
    )(flags, x, above, below, gain[:, None], shift[:, None], *stats)


def gather_wa(parts):
    n_wa = lax.axis_size("wa")
    pieces = {0: list(parts)}
    bit = n_wa // 2
    while bit:
        for k in sorted(pieces):
            pieces[k | bit] = [lax.ppermute(p, "wa", xor_pairs(n_wa, bit)) for p in pieces[k]]
        bit //= 2
    return [pieces[k] for k in range(n_wa)]


def prepared(kernel, ci, co):
    flat = kernel.reshape(TAPS, TAPS * ci, co)
    turned = jnp.transpose(flat, (2, 0, 1))
    depth = -(-TAPS * ci // 128) * 128
    turned = jnp.pad(turned, ((0, 0), (0, 0), (0, depth - TAPS * ci)))
    return turned.reshape(co, TAPS * depth)


def ring_order(n):
    return list(range(0, n, 2)) + list(range(n - 1, 0, -2))


def ring_blocks():
    n = lax.axis_size("row")
    r = lax.axis_index("row")
    place = jnp.where(r % 2 == 0, r // 2, n - 1 - r // 2)
    shifts = [0]
    for s in range(1, n // 2):
        shifts += [n - s, s]
    shifts.append(n // 2)
    at = (place + jnp.array(shifts, jnp.int32)) % n
    return jnp.where(2 * at < n, 2 * at, 2 * (n - at) - 1)


def ring(own, hold):
    n = lax.axis_size("row")
    order = ring_order(n)
    up = [(order[i], order[(i + 1) % n]) for i in range(n)]
    down = [(d, s) for s, d in up]
    chunks = [own]
    a = b = own
    for s in range(1, n // 2 + 1):
        if s in hold:
            a, b, _ = lax.optimization_barrier((a, b, hold[s]))
        if s == n // 2:
            half = own.shape[0] // 2
            a, b = a[:half], b[half:]
        a = lax.ppermute(a, "row", up)
        b = lax.ppermute(b, "row", down)
        chunks += [a, b]
    return chunks


def conv_body(early, n_chunks, n_wa, idx_ref, chunk_refs, act_refs, acc_ref, wbuf, abuf, xbuf, wsem, asem):
    rows, co, lanes = acc_ref.shape
    ci = abuf.shape[2]
    depth = xbuf.shape[1]
    per_shard = n_chunks // n_wa
    me = idx_ref[n_chunks]

    def piece_of(c):
        return (idx_ref[c] // per_shard) ^ me

    def mine(c):
        soon = jnp.logical_and(piece_of(c) < 2, c < n_chunks - 1)
        return soon if early else jnp.logical_not(soon)

    for c in range(n_chunks - 1 if early else n_chunks):

        @pl.when(mine(c))
        def _():
            if c < n_chunks - 1:
                pltpu.make_async_copy(chunk_refs[c], wbuf.at[c], wsem.at[c]).start()
            else:
                half = co // 2
                for i in range(2):
                    pltpu.make_async_copy(
                        chunk_refs[c + i], wbuf.at[c, pl.ds(i * half, half), :], wsem.at[c]
                    ).start()
            slot = piece_of(c) * per_shard + idx_ref[c] % per_shard
            for k in range(len(act_refs)):

                @pl.when(slot == k)
                def _():
                    pltpu.make_async_copy(act_refs[k], abuf.at[c], asem.at[c]).start()

    if depth > TAPS * ci:
        xbuf[:, TAPS * ci :, :] = jnp.zeros((rows + 2, depth - TAPS * ci, lanes), jnp.bfloat16)
    column = lax.broadcasted_iota(jnp.int32, (ci, lanes), 1) % WIDTH

    def step(c, carry):
        @pl.when(mine(c))
        def _():
            pltpu.make_async_copy(act_refs[0], abuf.at[c], asem.at[c]).wait()
            for r in range(rows + 2):
                v = abuf[c, r]
                zero = jnp.zeros_like(v)
                xbuf[r, 0:ci, :] = jnp.where(column == 0, zero, pltpu.roll(v, 1, 1))
                xbuf[r, ci : 2 * ci, :] = v
                xbuf[r, 2 * ci : 3 * ci, :] = jnp.where(column == WIDTH - 1, zero, pltpu.roll(v, lanes - 1, 1))
            pltpu.make_async_copy(chunk_refs[0], wbuf.at[c], wsem.at[c]).wait()
            for r in range(rows):
                panel = xbuf[r : r + TAPS].reshape(TAPS * depth, lanes)
                acc_ref[r] += jnp.dot(wbuf[c], panel, preferred_element_type=jnp.float32)

        return carry

    lax.fori_loop(0, n_chunks - 1 if early else n_chunks, step, 0)


def conv_part(early, idx, chunks, acts, acc, bias):
    n_wa = lax.axis_size("wa")
    n_chunks = lax.axis_size("row")
    rows, ci, lanes = acts[0].shape
    rows -= 2
    co, kdim = chunks[0].shape
    depth = kdim // TAPS
    n_in = len(chunks) + len(acts)

    def body(idx_ref, *refs):
        refs = list(refs)
        chunk_refs = refs[: len(chunks)]
        act_refs = refs[len(chunks) : n_in]
        rest = refs[n_in:]
        if early:
            acc_ref, *scratch = rest
            acc_ref[...] = jnp.zeros(acc_ref.shape, jnp.float32)
        else:
            acc_in, bias_ref, out_ref, acc_ref, *scratch = rest
            acc_ref[...] = acc_in[...] + bias_ref[...][None]
        conv_body(early, n_chunks, n_wa, idx_ref, chunk_refs, act_refs, acc_ref, *scratch)
        if not early:
            out_ref[...] = acc_ref[...].astype(jnp.bfloat16)

    any_spec = pl.BlockSpec(memory_space=pl.ANY)
    full = pl.BlockSpec(memory_space=pltpu.VMEM)
    in_specs = [pl.BlockSpec(memory_space=pltpu.SMEM)] + [any_spec] * n_in
    args = [idx] + chunks + acts
    scratch = []
    if not early:
        in_specs += [full, full]
        args += [acc, bias[:, None]]
        scratch.append(pltpu.VMEM((rows, co, lanes), jnp.float32))
    scratch += [
        pltpu.VMEM((n_chunks, co, kdim), jnp.bfloat16),
        pltpu.VMEM((n_chunks, rows + 2, ci, lanes), jnp.bfloat16),
        pltpu.VMEM((rows + 2, depth, lanes), jnp.bfloat16),
        pltpu.SemaphoreType.DMA((n_chunks,)),
        pltpu.SemaphoreType.DMA((n_chunks,)),
    ]
    return pl.pallas_call(
        body,
        in_specs=in_specs,
        out_specs=full,
        out_shape=jax.ShapeDtypeStruct((rows, co, lanes), jnp.float32 if early else jnp.bfloat16),
        scratch_shapes=scratch,
        compiler_params=params(),
        name="conv",
    )(*args)


def convolve(parts, chunks, idx, bias):
    pieces = gather_wa(parts)
    near = pieces[0] + pieces[1]
    every = [p for piece in pieces for p in piece]
    acc = conv_part(True, idx, chunks[:-2], near, None, None)
    return conv_part(False, idx, chunks, every, acc, bias)


def per_device(
    activations,
    gain_one,
    shift_one,
    kernel_one,
    bias_one,
    gain_two,
    shift_two,
    kernel_two,
    bias_two,
):
    co = activations.shape[1]
    ci = kernel_one.shape[4] // co
    idx = jnp.concatenate([ring_blocks(), lax.axis_index("wa").astype(jnp.int32)[None]])
    own_one = prepared(kernel_one, ci, co)
    own_two = prepared(kernel_two, ci, co)
    around = surroundings(activations)
    chunks_one = ring(own_one, {2: (around, own_two)})
    first = activate(activations, around, gain_one, shift_one)
    hidden = convolve(first, chunks_one, idx, bias_one)
    around = surroundings(hidden)
    chunks_two = ring(own_two, {2: around})
    second = activate(hidden, around, gain_two, shift_two)
    return convolve(second, chunks_two, idx, bias_two)


def solution(mesh):
    placed = (
        P("row", "wa", None),
        P("wa"),
        P("wa"),
        P(None, None, "row", "wa", None),
        P("wa"),
        P("wa"),
        P("wa"),
        P(None, None, "row", "wa", None),
        P("wa"),
    )

    return jax.shard_map(
        per_device, mesh=mesh, in_specs=placed, out_specs=P("row", "wa", None), check_vma=False
    )
```

```python
import jax
import jax.numpy as jnp
from jax import lax
from jax.experimental import pallas as pl
from jax.experimental.pallas import tpu as pltpu
from jax.sharding import PartitionSpec as P


C = 1280
GROUPS = 32
WIDTH = 32
GROUP_SIZE = C // GROUPS
TAPS = 3
EPS = 1e-05
VMEM_LIMIT = 60 * 1024 * 1024


def params(**extra):
    return pltpu.CompilerParams(vmem_limit_bytes=VMEM_LIMIT, **extra)


def xor_pairs(count, bit):
    return [(i, i ^ bit) for i in range(count)]


def image_select(lanes, images=128):
    lane = lax.broadcasted_iota(jnp.int32, (lanes, images), 0) // WIDTH
    return (lane == lax.broadcasted_iota(jnp.int32, (lanes, images), 1)).astype(jnp.float32)


def image_sum(value, select):
    return jnp.dot(value, select, precision=lax.Precision.HIGHEST, preferred_element_type=jnp.float32)


def image_spread(value, select):
    return lax.dot_general(
        value, select, (((1,), (1,)), ((), ())), precision=lax.Precision.HIGHEST, preferred_element_type=jnp.float32
    )


def stats_into(x_ref, out_ref, total_ref):
    rows, chans, lanes = x_ref.shape
    groups = chans // GROUP_SIZE
    count = rows * GROUP_SIZE * WIDTH
    select = image_select(lanes)
    spans = [slice(g * GROUP_SIZE, (g + 1) * GROUP_SIZE) for g in range(groups)]
    for g in range(groups):
        part = x_ref[:, spans[g], :].astype(jnp.float32)
        total_ref[g : g + 1, :] = jnp.sum(jnp.sum(part, axis=0), axis=0, keepdims=True)
    mean = image_sum(total_ref[...], select) / count
    out_ref[0] = mean
    wide = image_spread(mean, select)
    for g in range(groups):
        off = x_ref[:, spans[g], :].astype(jnp.float32) - wide[None, g : g + 1, :]
        total_ref[g : g + 1, :] = jnp.sum(jnp.sum(off * off, axis=0), axis=0, keepdims=True)
    out_ref[1] = image_sum(total_ref[...], select)


def edge_shapes(x_shape):
    _, chans, lanes = x_shape
    edge = jax.ShapeDtypeStruct((1, chans, lanes), jnp.bfloat16)
    return [edge, edge, jax.ShapeDtypeStruct((2, chans // GROUP_SIZE, 128), jnp.float32)]


def summary_of(x):
    def body(x_ref, top_ref, bottom_ref, stats_ref, total_ref):
        rows = x_ref.shape[0]
        top_ref[0] = x_ref[0]
        bottom_ref[0] = x_ref[rows - 1]
        stats_into(x_ref, stats_ref, total_ref)

    return pl.pallas_call(
        body,
        out_shape=edge_shapes(x.shape),
        scratch_shapes=[pltpu.VMEM((x.shape[1] // GROUP_SIZE, x.shape[2]), jnp.float32)],
        compiler_params=params(),
        name="stats",
    )(x)


def surroundings(summary):
    n_row = lax.axis_size("row")
    top, bottom, stats = summary
    above = lax.ppermute(bottom, "row", [(i, i + 1) for i in range(n_row - 1)])
    below = lax.ppermute(top, "row", [(i + 1, i) for i in range(n_row - 1)])
    every = [stats]
    for k in range(1, n_row):
        every.append(lax.ppermute(stats, "row", xor_pairs(n_row, k)))
    return (above, below), every


def norm_body(count, n_row, column, flag_ref, x_ref, above_ref, below_ref, columns_ref, *refs):
    stats_refs = refs[:n_row]
    out_refs = refs[n_row:]
    rows, chans, lanes = x_ref.shape
    groups = chans // GROUP_SIZE
    width = out_refs[0].shape[1]
    select = image_select(lanes)
    center = sum(ref[0] for ref in stats_refs) / n_row
    square = sum(ref[1] for ref in stats_refs) + count * sum(jnp.square(ref[0] - center) for ref in stats_refs)
    scale = lax.rsqrt(square / (count * n_row) + EPS)
    wide_center = image_spread(center, select)
    wide_scale = image_spread(scale, select)
    for g in range(groups):
        span = slice(g * GROUP_SIZE, (g + 1) * GROUP_SIZE)
        out_ref = out_refs[g * GROUP_SIZE // width]
        start = g * GROUP_SIZE % width
        mean = wide_center[g : g + 1, :]
        inv = wide_scale[g : g + 1, :]
        gain = columns_ref[span, column : column + 1]
        shift = columns_ref[span, column + 1 : column + 2]

        def act(value):
            v = (value.astype(jnp.float32) - mean) * inv * gain + shift
            return v / (1.0 + jnp.exp(-v))

        here = slice(start, start + GROUP_SIZE)
        out_ref[0, here, :] = (act(above_ref[0, span, :]) * flag_ref[0]).astype(jnp.bfloat16)
        for r in range(rows):
            out_ref[r + 1, here, :] = act(x_ref[r, span, :]).astype(jnp.bfloat16)
        out_ref[rows + 1, here, :] = (act(below_ref[0, span, :]) * flag_ref[1]).astype(jnp.bfloat16)


def activate(x, around, columns, column):
    n_row = lax.axis_size("row")
    rows, chans, lanes = x.shape
    ci = C // n_row
    count = rows * GROUP_SIZE * WIDTH
    (above, below), stats = around
    r = lax.axis_index("row")
    flags = jnp.stack([r > 0, r < n_row - 1]).astype(jnp.float32)
    vmem = pl.BlockSpec(memory_space=pltpu.VMEM)
    return pl.pallas_call(
        lambda *refs: norm_body(count, n_row, column, *refs),
        in_specs=[pl.BlockSpec(memory_space=pltpu.SMEM)] + [vmem] * (4 + n_row),
        out_shape=[jax.ShapeDtypeStruct((rows + 2, ci, lanes), jnp.bfloat16)] * (chans // ci),
        compiler_params=params(),
        name="norm",
    )(flags, x, above, below, columns, *stats)


def gather_wa(parts):
    n_wa = lax.axis_size("wa")
    pieces = {0: list(parts)}
    bit = n_wa // 2
    while bit:
        for k in sorted(pieces):
            pieces[k | bit] = []
            for part in pieces[k]:
                pieces[k | bit].append(lax.ppermute(part, "wa", xor_pairs(n_wa, bit)))
        bit //= 2
    return [pieces[k] for k in range(n_wa)]


def prepared(kernel, ci, co):
    flat = kernel.reshape(TAPS, TAPS * ci, co)
    turned = jnp.transpose(flat, (2, 0, 1))
    depth = -(-TAPS * ci // 128) * 128
    turned = jnp.pad(turned, ((0, 0), (0, 0), (0, depth - TAPS * ci)))
    return turned.reshape(co, TAPS * depth)


def ring_order(n):
    return list(range(0, n, 2)) + list(range(n - 1, 0, -2))


def ring_blocks():
    n = lax.axis_size("row")
    r = lax.axis_index("row")
    place = jnp.where(r % 2 == 0, r // 2, n - 1 - r // 2)
    shifts = [0]
    for s in range(1, n // 2):
        shifts += [n - s, s]
    shifts.append(n // 2)
    at = (place + jnp.array(shifts, jnp.int32)) % n
    return jnp.where(2 * at < n, 2 * at, 2 * (n - at) - 1)


def ring(own, hold):
    n = lax.axis_size("row")
    order = ring_order(n)
    up = [(order[i], order[(i + 1) % n]) for i in range(n)]
    down = [(d, s) for s, d in up]
    chunks = [own]
    a = b = own
    for s in range(1, n // 2 + 1):
        if s in hold:
            a, b, _ = lax.optimization_barrier((a, b, hold[s]))
        if s == n // 2:
            half = own.shape[0] // 2
            a, b = a[:half], b[half:]
        a = lax.ppermute(a, "row", up)
        b = lax.ppermute(b, "row", down)
        chunks += [a, b]
    return chunks


def conv_body(stage, before, n_chunks, n_wa, idx_ref, chunk_refs, act_refs, acc_ref, wbuf, abuf, xbuf, order, wsem, asem):
    rows, co, lanes = acc_ref.shape
    ci = abuf.shape[2]
    depth = xbuf.shape[2]
    per_shard = n_chunks // n_wa
    me = idx_ref[n_chunks]
    buffers = wbuf.shape[0]

    def piece_of(c):
        return (idx_ref[c] // per_shard) ^ me

    def there(c, at):
        if at is None or c >= at[0]:
            return jnp.bool_(False)
        return piece_of(c) < 2 if at[1] else jnp.bool_(True)

    last = stage[0] == n_chunks
    count = jnp.int32(0)
    for c in range(stage[0]):
        mine = jnp.logical_and(there(c, stage), jnp.logical_not(there(c, before)))

        @pl.when(mine)
        def _():
            order[count] = c

        count += mine.astype(jnp.int32)

    def start(i):
        @pl.when(i < count)
        def _():
            slot = i % buffers
            chunk = order[i]
            act = piece_of(chunk) * per_shard + idx_ref[chunk] % per_shard
            for k in range(len(act_refs)):

                @pl.when(act == k)
                def _():
                    pltpu.make_async_copy(act_refs[k], abuf.at[slot], asem.at[slot]).start()

            for c in range(min(stage[0], n_chunks - 1)):

                @pl.when(chunk == c)
                def _():
                    pltpu.make_async_copy(chunk_refs[c], wbuf.at[slot], wsem.at[slot]).start()

            if last:

                @pl.when(chunk == n_chunks - 1)
                def _():
                    half = co // 2
                    for k in range(2):
                        pltpu.make_async_copy(
                            chunk_refs[n_chunks - 1 + k], wbuf.at[slot, pl.ds(k * half, half), :], wsem.at[slot]
                        ).start()

    def acts_ready(i):
        @pl.when(i < count)
        def _():
            slot = i % buffers
            pltpu.make_async_copy(act_refs[0], abuf.at[slot], asem.at[slot]).wait()

    column = lax.broadcasted_iota(jnp.int32, (ci, lanes), 1) % WIDTH

    def build(i):
        for r in range(rows + 2):
            v = abuf[i % buffers, r]
            zero = jnp.zeros_like(v)
            xbuf[i % 2, r, 0:ci, :] = jnp.where(column == 0, zero, pltpu.roll(v, 1, 1))
            xbuf[i % 2, r, ci : 2 * ci, :] = v
            xbuf[i % 2, r, 2 * ci : 3 * ci, :] = jnp.where(column == WIDTH - 1, zero, pltpu.roll(v, lanes - 1, 1))

    def step(i, carry):
        start(i + 2)
        acts_ready(i + 1)
        pltpu.make_async_copy(chunk_refs[0], wbuf.at[i % buffers], wsem.at[i % buffers]).wait()
        build(i + 1)
        for r in range(rows):
            panel = xbuf[i % 2, r : r + TAPS].reshape(TAPS * depth, lanes)
            acc_ref[r] += jnp.dot(wbuf[i % buffers], panel, preferred_element_type=jnp.float32)
        return carry

    start(jnp.int32(0))
    start(jnp.int32(1))
    if depth > TAPS * ci:
        xbuf[:, :, TAPS * ci :, :] = jnp.zeros((2, rows + 2, depth - TAPS * ci, lanes), jnp.bfloat16)
    acts_ready(jnp.int32(0))
    build(jnp.int32(0))
    lax.fori_loop(0, count, step, 0)


def conv_part(stage, before, idx, chunks, acts, acc, columns, column, summary):
    n_wa = lax.axis_size("wa")
    n_chunks = lax.axis_size("row")
    last = stage[0] == n_chunks
    rows, ci, lanes = acts[0].shape
    rows -= 2
    co, kdim = chunks[0].shape
    depth = kdim // TAPS
    n_in = len(chunks) + len(acts)
    shape = (rows, co, lanes)

    def body(idx_ref, *refs):
        refs = list(refs)
        chunk_refs = refs[: len(chunks)]
        act_refs = refs[len(chunks) : n_in]
        rest = refs[n_in:]
        acc_in = rest.pop(0) if before is not None else None
        columns_ref = rest.pop(0) if last else None
        out_ref = rest.pop(0)
        summary_refs = [rest.pop(0) for _ in range(3)] if summary else None
        acc_ref = rest.pop(0) if last else out_ref
        total_ref = rest.pop(0) if summary else None
        value = jnp.zeros(shape, jnp.float32) if before is None else acc_in[...]
        acc_ref[...] = value + columns_ref[:, column : column + 1][None] if last else value
        conv_body(stage, before, n_chunks, n_wa, idx_ref, chunk_refs, act_refs, acc_ref, *rest)
        if last:
            out_ref[...] = acc_ref[...].astype(jnp.bfloat16)
        if summary:
            summary_refs[0][0] = out_ref[0]
            summary_refs[1][0] = out_ref[rows - 1]
            stats_into(out_ref, summary_refs[2], total_ref)

    any_spec = pl.BlockSpec(memory_space=pl.ANY)
    full = pl.BlockSpec(memory_space=pltpu.VMEM)
    in_specs = [pl.BlockSpec(memory_space=pltpu.SMEM)] + [any_spec] * n_in
    args = [idx] + list(chunks) + list(acts)
    scratch = []
    if before is not None:
        in_specs.append(full)
        args.append(acc)
    if last:
        in_specs.append(full)
        args.append(columns)
        scratch.append(pltpu.VMEM(shape, jnp.float32))
    if summary:
        scratch.append(pltpu.VMEM((co // GROUP_SIZE, lanes), jnp.float32))
    scratch += [
        pltpu.VMEM((3, co, kdim), jnp.bfloat16),
        pltpu.VMEM((3, rows + 2, ci, lanes), jnp.bfloat16),
        pltpu.VMEM((2, rows + 2, depth, lanes), jnp.bfloat16),
        pltpu.SMEM((n_chunks,), jnp.int32),
        pltpu.SemaphoreType.DMA((3,)),
        pltpu.SemaphoreType.DMA((3,)),
    ]
    outs = [jax.ShapeDtypeStruct(shape, jnp.bfloat16 if last else jnp.float32)]
    outs += edge_shapes(shape) if summary else []
    result = pl.pallas_call(
        body,
        in_specs=in_specs,
        out_specs=[full] * len(outs),
        out_shape=outs,
        scratch_shapes=scratch,
        compiler_params=params(),
        name="conv",
    )(*args)
    return result if summary else result[0]


def convolve(parts, chunks, idx, columns, column, summary):
    n = lax.axis_size("row")
    pieces = gather_wa(parts)
    near = pieces[0] + pieces[1]
    every = [p for piece in pieces for p in piece]
    stages = [(n - 3, True), (n - 1, False), (n, False)]
    acc = None
    before = None
    for stage in stages:
        last = stage[0] == n
        acts = near if stage[1] else every
        taken = chunks if last else chunks[: stage[0]]
        acc = conv_part(stage, before, idx, taken, acts, acc, columns, column, summary and last)
        before = stage
    return acc


def per_device(
    activations,
    gain_one,
    shift_one,
    kernel_one,
    bias_one,
    gain_two,
    shift_two,
    kernel_two,
    bias_two,
):
    co = activations.shape[1]
    ci = kernel_one.shape[4] // co
    idx = jnp.concatenate([ring_blocks(), lax.axis_index("wa").astype(jnp.int32)[None]])
    own_one = prepared(kernel_one, ci, co)
    own_two = prepared(kernel_two, ci, co)
    columns = jnp.stack([gain_one, shift_one, bias_one, gain_two, shift_two, bias_two], axis=1)
    idx, own_two, columns = lax.optimization_barrier((idx, own_two, columns))
    around = surroundings(summary_of(activations))
    chunks_one = ring(own_one, {2: (idx, own_two, columns)})
    first = activate(activations, around, columns, 0)
    hidden, *summary = convolve(first, chunks_one, idx, columns, 2, True)
    around = surroundings(summary)
    chunks_two = ring(own_two, {})
    second = activate(hidden, around, columns, 3)
    return convolve(second, chunks_two, idx, columns, 5, False)


def solution(mesh):
    placed = (
        P("row", "wa", None),
        P("wa"),
        P("wa"),
        P(None, None, "row", "wa", None),
        P("wa"),
        P("wa"),
        P("wa"),
        P(None, None, "row", "wa", None),
        P("wa"),
    )

    return jax.shard_map(per_device, mesh=mesh, in_specs=placed, out_specs=P("row", "wa", None), check_vma=False)
```
